512 devices in a mesh: feat: 8 (over z_lo), lat: 64 (over y, z_hi, x, core).
Axes of the slice: x: 4, y: 4, z: 16 (z_hi: 2, z_lo: 8; z = z_hi * 8 + z_lo), core: 2. Of those that a mesh axis runs over, the one named last changes fastest.
Arguments:
- acts: bfloat16 [2, 512, 4096], P(None, 'lat', 'feat'), may hold values from -6 to 6
- weight: bfloat16 [2, 4096, 65536], P(None, 'feat', 'lat'), may hold values from -0.0625 to 0.0625
- enc_bias: float32 [65536], P('lat'), may hold values from -1 to 0.5
- dec_bias: float32 [2, 4096], P(None, 'feat'), may hold values from -1 to 1
Outputs:
- grad_weight: bfloat16 [2, 4096, 65536], P(None, 'feat', 'lat')
- grad_enc_bias: float32 [65536], P('lat')
- grad_dec_bias: float32 [2, 4096], P(None, 'feat')
The draws below stay inside these ranges and needn't reach their ends.
All inputs are finite; a program needn't handle non-finite values.
Results may differ from the reference program's by a relative error of at most 0.0085.
Values may be sent and summed in bfloat16 or wider, within the bound.
A program may use at most 64 MiB of HBM per device.

```python
import math
import jax
import jax.numpy as jnp
from jax import lax

D = 4096
LAT_DEV = 1024
LATENTS = 65536
ROWS = 512
N_FEAT = 8
N_LAT = 64


def block_levels(key, extent, split, least, largest):
    loudness, own = 1.0, jax.random.fold_in(key, 6)
    for axis_at, blocks in split:
        heights = jnp.exp(jax.random.uniform(jax.random.fold_in(own, axis_at), (blocks,), jnp.float32, least / len(split), largest / len(split)))
        loudness = loudness * jnp.repeat(heights, extent[axis_at] // blocks).reshape([-1 if axis == axis_at else 1 for axis in range(len(extent))])
    return loudness


def bell_draw(key, extent, deviation, limit, cuts=(), kind=jnp.bfloat16):
    gain = block_levels(key, extent, cuts, -0.22, 0.18) if cuts else 1.0
    drawn = jax.random.normal(key, extent, jnp.float32) * deviation * gain
    return jnp.minimum(jnp.maximum(drawn, -limit), limit).astype(kind)


def setup_inputs(seed: int = 0) -> dict:
    key_of = jax.random.split(jax.random.key(seed), 5)
    return {
        "acts": bell_draw(key_of[0], (2, ROWS, D), 1.0, 6.0, ((1, 64), (2, 8))),
        "weight": bell_draw(key_of[1], (2, D, LATENTS), (2 * D) ** -0.5, 0.0625, ((1, 8), (2, 64))),
        "enc_bias": jnp.clip(-1.0 + 1.5 * jax.random.uniform(key_of[2], (LATENTS,), jnp.float32) ** block_levels(key_of[2], (LATENTS,), ((0, 64),), -0.2, 0.2), -1.0, 0.5),
        "dec_bias": jnp.clip(jax.random.uniform(key_of[3], (2, D), jnp.float32, -1.0, 1.0) * block_levels(key_of[3], (2, D), ((1, 8),), -0.4, 0.0), -1.0, 1.0),
    }


def grouped(left, right):
    part = left.shape[2] // N_FEAT
    total = jnp.zeros((left.shape[1], right.shape[2]), jnp.float32)
    for group in range(N_FEAT):
        low = group * part
        term = jnp.dot(left[0, :, low:low + part], right[0, low:low + part, :], preferred_element_type=jnp.float32)
        term = term + jnp.dot(left[1, :, low:low + part], right[1, low:low + part, :], preferred_element_type=jnp.float32)
        rounded = lax.optimization_barrier(term.astype(jnp.bfloat16))
        total = total + rounded.astype(jnp.float32)
    return total

def reference(acts, weight, enc_bias, dec_bias):
    width = acts.shape[2]
    lats = weight.shape[2]
    scale = math.sqrt(2.0 * width / lats)
    starts = jnp.arange(N_LAT, dtype=jnp.int32) * LAT_DEV

    def forward(carry, start):
        block = lax.dynamic_slice_in_dim(weight, start, LAT_DEV, 2)
        bias_block = lax.dynamic_slice_in_dim(enc_bias, start, LAT_DEV, 0)
        pre = grouped(acts, block) + bias_block
        latents = jax.nn.softplus(pre).astype(jnp.bfloat16)
        first = jnp.dot(latents, block[0].T, preferred_element_type=jnp.float32)
        second = jnp.dot(latents, block[1].T, preferred_element_type=jnp.float32)
        return (carry + jnp.stack([first, second]), pre)
    zeros = jnp.zeros((2, acts.shape[1], width), jnp.float32)
    summed, pres = lax.scan(forward, zeros, starts)
    resid = scale * summed + dec_bias[:, None, :] - acts.astype(jnp.float32)
    grad_dec_bias = lax.optimization_barrier(jnp.sum(resid, axis=1))
    resid_b = resid.astype(jnp.bfloat16)

    def backward(carry, inputs):
        start, pre = inputs
        block = lax.dynamic_slice_in_dim(weight, start, LAT_DEV, 2)
        latents = jax.nn.softplus(pre).astype(jnp.bfloat16)
        grad_pre = scale * grouped(resid_b, block) * jax.nn.sigmoid(pre)
        bias_part = lax.optimization_barrier(jnp.sum(grad_pre, axis=0))
        grad_pre_b = grad_pre.astype(jnp.bfloat16)
        outs = []
        for model in range(2):
            enc_term = jnp.dot(acts[model].T, grad_pre_b, preferred_element_type=jnp.float32)
            dec_term = jnp.dot(resid_b[model].T, latents, preferred_element_type=jnp.float32)
            outs.append((enc_term + scale * dec_term).astype(jnp.bfloat16))
        return (carry, (jnp.stack(outs), bias_part))
    unused, (blocks, bias_blocks) = lax.scan(backward, jnp.zeros((), jnp.float32), (starts, pres))
    grad_weight = jnp.transpose(blocks, (1, 2, 0, 3)).reshape(2, width, lats)
    grad_enc_bias = bias_blocks.reshape(lats)
    return (grad_weight, grad_enc_bias, grad_dec_bias)
```

```python
import functools
import math

import jax
import jax.numpy as jnp
from jax import lax
from jax.experimental import pallas as pl
from jax.experimental.pallas import tpu as pltpu
from jax.sharding import Mesh
from jax.sharding import PartitionSpec as P

LAT = ("lat_0", "lat_1", "lat_2", "lat_3")
AXES = ("feat", *LAT)
BF16, F32 = jnp.bfloat16, jnp.float32
TILE = 16
SKEW = 5


def chain_kernel(
    sizes, scale, a_ref, w_hbm, eb_ref, db_ref, gw_ref, geb_ref, gdb_ref,
    w_ref, abuf, xs, prod, sig, lats, grads, res, sr, ss, tl, ts, sr2, ss2, tl2, ts2,
    half_out, half_in, half_own, part_out, part_in, pair_out, pair_in, acc, gacc, gebuf,
    w_sem, h_sem, xy_sem, core_sem, line_sem, line2_sem, geb_send, geb_recv,
):
    nf, ny, _, nx, _ = sizes
    nq = ny * nx
    nt = 2 * nq
    width, nlat = w_ref.shape[1], w_ref.shape[2]
    f, y, h, x, c = (lax.axis_index(name) for name in AXES)
    q = y * nx + x
    mine, base, other_base = c * nq + q, c * nq, (1 - c) * nq
    mid = (nf - 1) // 2
    partner, sibling = (f, y, 1 - h, x, c), (f, y, h, x, 1 - c)
    after, before = (jnp.minimum(f + 1, nf - 1), y, h, x, c), (jnp.maximum(f - 1, 0), y, h, x, c)
    offsets = [(dy, dx) for dy in range(ny) for dx in range(nx) if dy or dx]

    def at_offset(dy, dx):
        return lax.rem(y + dy + ny, ny), lax.rem(x + dx + nx, nx)

    def remote(src, dst, send, recv, to):
        return pltpu.make_async_remote_copy(
            src_ref=src, dst_ref=dst, send_sem=send, recv_sem=recv,
            device_id=to, device_id_type=pl.DeviceIdType.MESH,
        )

    w_copy = pltpu.make_async_copy(w_hbm, w_ref, w_sem)
    w_copy.start()

    barrier = pltpu.get_barrier_semaphore()

    def greet(to):
        pl.semaphore_signal(barrier, inc=1, device_id=to, device_id_type=pl.DeviceIdType.MESH)

    greet(partner)
    greet(sibling)
    for dy, dx in offsets:
        py, px = at_offset(dy, dx)
        greet((f, py, h, px, c))

    @pl.when(f > 0)
    def _():
        greet(before)

    @pl.when(f < nf - 1)
    def _():
        greet(after)

    @pl.when(f != mid)
    def _():
        greet((mid, y, h, x, c))

    beside = (f > 0).astype(jnp.int32) + (f < nf - 1).astype(jnp.int32)
    listeners = (nf - 1) * (f == mid).astype(jnp.int32)
    pl.semaphore_wait(barrier, 2 + len(offsets) + beside + listeners)

    def swap_along_z(src, dst, at):
        copy = remote(src, dst, h_sem.at[0, at], h_sem.at[1, at], partner)
        copy.start()
        copy.wait()

    def gathered(buf, at):
        sends, passed = [], []

        def pass_on(tile, source):
            copy = remote(
                buf.at[tile], buf.at[tile], core_sem.at[0, at, source], core_sem.at[1, at, source], sibling
            )
            copy.start()
            passed.append(copy)

        for number, (dy, dx) in enumerate(offsets):
            py, px = at_offset(dy, dx)
            copy = remote(
                buf.at[mine], buf.at[mine], xy_sem.at[0, at, number], xy_sem.at[1, at, q], (f, py, h, px, c)
            )
            copy.start()
            sends.append(copy)
        pass_on(mine, q)
        for dy, dx in offsets:
            py, px = at_offset(-dy, -dx)
            source = py * nx + px
            remote(
                buf.at[mine], buf.at[base + source], xy_sem.at[0, at, 0], xy_sem.at[1, at, source], sibling
            ).wait_recv()
            pass_on(base + source, source)
        for copy in sends + passed:
            copy.wait_send()
        for source in range(nq):
            remote(
                buf.at[mine], buf.at[other_base + source], core_sem.at[0, at, 0], core_sem.at[1, at, source], sibling
            ).wait_recv()

    def products(left):
        per = min(16, nt)
        columns = 256

        @pl.loop(0, nt // per)
        def _(group):
            tiles = pl.ds(group * per, per)

            @pl.loop(0, nlat // columns)
            def _(block):
                cols = pl.ds(pl.multiple_of(block * columns, columns), columns)
                total = jnp.dot(
                    left[tiles, 0].reshape(per * TILE, width), w_ref[0, :, cols], preferred_element_type=F32
                )
                total = total + jnp.dot(
                    left[tiles, 1].reshape(per * TILE, width), w_ref[1, :, cols], preferred_element_type=F32
                )
                prod[tiles, :, cols] = total.reshape(per, TILE, columns)

    def chained(right_in, right_out, left_in, left_out, sems, on_total, on_step):
        last = nf - 1

        @pl.when(f == 0)
        def _():
            right_in[...] = jnp.zeros_like(right_in)

        @pl.when(f == last)
        def _():
            left_in[...] = jnp.zeros_like(left_in)

        def to_right(k):
            return remote(right_out.at[k], right_in.at[k], sems.at[0, k], sems.at[1, k], after)

        def to_left(k):
            return remote(left_out.at[k], left_in.at[k], sems.at[2, k], sems.at[3, k], before)

        lag = jnp.maximum(f, last - f)

        @pl.loop(0, nt + SKEW * last)
        def _(step):
            right, left, done = step - SKEW * f, step - SKEW * (last - f), step - SKEW * lag

            @pl.when((right >= 0) & (right < nt))
            def _():
                @pl.when(f > 0)
                def _():
                    to_right(right).wait_recv()

                @pl.when(f < last)
                def _():
                    right_out[right] = (prod[right] + right_in[right].astype(F32)).astype(BF16)
                    to_right(right).start()

            @pl.when((left >= 0) & (left < nt))
            def _():
                @pl.when(f < last)
                def _():
                    to_left(left).wait_recv()

                @pl.when(f > 0)
                def _():
                    left_out[left] = (prod[left] + left_in[left].astype(F32)).astype(BF16)
                    to_left(left).start()

            @pl.when((done >= 0) & (done < nt))
            def _():
                on_total(done, prod[done] + right_in[done].astype(F32) + left_in[done].astype(F32))

            on_step(step)

        @pl.loop(0, nt)
        def _(k):
            @pl.when(f < last)
            def _():
                to_right(k).wait_send()

            @pl.when(f > 0)
            def _():
                to_left(k).wait_send()

    swap_along_z(a_ref, abuf, 0)
    own, far = a_ref[...].astype(F32), abuf[...].astype(F32)
    low, high = jnp.where(h == 0, own, far), jnp.where(h == 0, far, own)
    rows = TILE // 2
    for m in range(2):
        part = slice(m * rows, (m + 1) * rows)
        xs[mine, m] = jnp.concatenate([low[part], high[part]], axis=0).astype(BF16)
    gathered(xs, 0)

    w_copy.wait()
    products(xs)

    def activate(k, total):
        pre = total + eb_ref[...]
        fall = jnp.exp(-jnp.abs(pre))
        lats[k] = (jnp.maximum(pre, 0.0) + jnp.log1p(fall)).astype(BF16)
        sig[k] = jnp.where(pre >= 0, 1.0, fall) / (1.0 + fall)

    chained(sr, ss, tl, ts, line_sem, activate, lambda step: None)

    per = min(8, nq)

    def terms(tile, m):
        return lax.dot_general(
            lats[pl.ds(tile, per)].reshape(per * TILE, nlat), w_ref[m],
            (((1,), (1,)), ((), ())), preferred_element_type=F32,
        ).reshape(per, TILE, width)

    @pl.loop(0, nq // per)
    def _(group):
        for m in range(2):
            half_out[pl.ds(group * per, per), m] = terms(other_base + group * per, m).astype(BF16)

    half_copy = remote(half_out, half_in, h_sem.at[0, 2], h_sem.at[1, 2], sibling)
    half_copy.start()

    @pl.loop(0, nq // per)
    def _(group):
        for m in range(2):
            half_own[pl.ds(group * per, per), m] = terms(base + group * per, m)

    half_copy.wait()
    sends = []
    for number, (dy, dx) in enumerate(offsets):
        py, px = at_offset(dy, dx)
        owner = py * nx + px
        part_out[number] = (half_own[owner] + half_in[owner].astype(F32)).astype(BF16)
        copy = remote(
            part_out.at[number], part_in.at[number], xy_sem.at[0, 2, number], xy_sem.at[1, 2, number], (f, py, h, px, c)
        )
        copy.start()
        sends.append(copy)
    total = half_own[q] + half_in[q].astype(F32)
    for number, copy in enumerate(sends):
        copy.wait_recv()
        total = total + part_in[number].astype(F32)
    pair_out[...] = total.astype(BF16)
    swap_along_z(pair_out, pair_in, 1)
    summed = pair_out[...].astype(F32) + pair_in[...].astype(F32)
    res[mine] = (scale * summed + db_ref[...] - xs[mine].astype(F32)).astype(BF16)
    gathered(res, 1)
    for copy in sends:
        copy.wait_send()

    products(res)
    gacc[...] = jnp.zeros_like(gacc)
    channels, columns = 128, 256
    across = nlat // columns
    along = width // channels

    def blocks_of(number):
        chan = pl.ds(pl.multiple_of(lax.rem(number // across, along) * channels, channels), channels)
        cols = pl.ds(pl.multiple_of(lax.rem(number, across) * columns, columns), columns)
        return number // (across * along), chan, cols

    def over_rows(left, m, chan, right, cols):
        return lax.dot_general(
            left[:, m, :, chan].reshape(nt * TILE, channels), right[:, :, cols].reshape(nt * TILE, columns),
            (((0,), (0,)), ((), ())), preferred_element_type=F32,
        )

    def dec_block(step):
        @pl.when(step < 2 * across * along)
        def _():
            m, chan, cols = blocks_of(step)
            acc[m, chan, cols] = scale * over_rows(res, m, chan, lats, cols)

    def finish(k, total):
        grad = scale * total * sig[k]
        grads[k] = grad.astype(BF16)
        gacc[...] += grad

    chained(sr2, ss2, tl2, ts2, line2_sem, finish, dec_block)

    first = 2 * across * along - (nt + SKEW * (nf - 1))
    if first > 0:
        @pl.loop(nt + SKEW * (nf - 1), 2 * across * along)
        def _(number):
            dec_block(number)

    def to_chip(ahead):
        return remote(
            gebuf, gebuf, geb_send.at[ahead], geb_recv.at[0], (lax.rem(mid + ahead, nf), y, h, x, c)
        )

    @pl.when(f == mid)
    def _():
        gebuf[...] = jnp.broadcast_to(jnp.sum(gacc[...], axis=0, keepdims=True), gebuf.shape)
        for ahead in range(1, nf):
            to_chip(ahead).start()

    gdb_ref[...] = jnp.sum(jnp.sum(res[...].astype(F32), axis=0), axis=1, keepdims=True)

    @pl.loop(0, 2 * across * along)
    def _(number):
        m, chan, cols = blocks_of(number)
        gw_ref[m, chan, cols] = (over_rows(xs, m, chan, grads, cols) + acc[m, chan, cols]).astype(BF16)

    @pl.when(f == mid)
    def _():
        for ahead in range(1, nf):
            to_chip(ahead).wait_send()

    @pl.when(f != mid)
    def _():
        to_chip(1).wait_recv()

    geb_ref[...] = gebuf[0:1]


def on_device(sizes, acts, weight, enc_bias, dec_bias):
    nf, ny, nh, nx, nc = sizes
    lat_count = ny * nh * nx * nc
    _, width, nlat = weight.shape
    scale = math.sqrt(2.0 * (width * nf) / (nlat * lat_count))
    nq = ny * nx
    nt = 2 * nq
    vmem = pltpu.VMEM
    tiles = vmem((nt, 2, TILE, width), BF16)
    chunk = vmem((nt, TILE, nlat), BF16)
    wide = vmem((nt, TILE, nlat), F32)
    half = vmem((nq, 2, TILE, width), BF16)
    pair = vmem((2, TILE, width), BF16)
    parts = vmem((max(nq - 1, 1), 2, TILE, width), BF16)
    dma = pltpu.SemaphoreType.DMA
    whole = pl.BlockSpec(memory_space=pltpu.VMEM)
    grad_weight, grad_enc, grad_dec = pl.pallas_call(
        functools.partial(chain_kernel, sizes, scale),
        out_shape=(
            jax.ShapeDtypeStruct((2, width, nlat), BF16),
            jax.ShapeDtypeStruct((1, nlat), F32),
            jax.ShapeDtypeStruct((2, 1, width), F32),
        ),
        in_specs=[whole, pl.BlockSpec(memory_space=pl.ANY), whole, whole],
        out_specs=(whole, whole, whole),
        scratch_shapes=[
            vmem((2, width, nlat), BF16), vmem((TILE, width), BF16),
            tiles, wide, wide, chunk, chunk, tiles,
            *([chunk] * 8),
            half, half, vmem((nq, 2, TILE, width), F32), parts, parts, pair, pair,
            vmem((2, width, nlat), F32), vmem((TILE, nlat), F32), vmem((8, nlat), F32),
            dma, dma((2, 3)), dma((2, 3, max(nq, 1))), dma((2, 2, nq)), dma((4, nt)), dma((4, nt)),
            dma((nf,)), dma((1,)),
        ],
        compiler_params=pltpu.CompilerParams(
            collective_id=0, has_side_effects=True, vmem_limit_bytes=60 * 1024 * 1024
        ),
        name="crosscoder_step",
    )(acts.reshape(TILE, width), weight, enc_bias.reshape(1, nlat), dec_bias.reshape(2, 1, width))
    return grad_weight, grad_enc.reshape(nlat), grad_dec.reshape(2, width)


def solution(mesh):
    shape = dict(mesh.shape)
    if shape["lat"] == 64:
        sizes = (shape["feat"], 4, 2, 4, 2)
    else:
        sizes = (shape["feat"], 1, 2, shape["lat"] // 4, 2)
    torus = Mesh(mesh.devices.reshape(sizes), AXES)
    in_specs = (P(None, LAT, "feat"), P(None, "feat", LAT), P(LAT), P(None, "feat"))
    out_specs = (P(None, "feat", LAT), P(LAT), P(None, "feat"))
    return jax.shard_map(
        functools.partial(on_device, sizes),
        mesh=torus, in_specs=in_specs, out_specs=out_specs, check_vma=False,
    )
```

```python
import functools
import math

import jax
import jax.numpy as jnp
from jax import lax
from jax.experimental import pallas as pl
from jax.experimental.pallas import tpu as pltpu
from jax.sharding import Mesh
from jax.sharding import PartitionSpec as P

LAT = ("lat_0", "lat_1", "lat_2", "lat_3")
AXES = ("feat", *LAT)
BF16, F32 = jnp.bfloat16, jnp.float32
TILE = 16
SKEW = 5
SCATTER_AT, PAIR_AT = 3, 12
RESID_AT, COLLECT_BEFORE = 5, 2


def chain_kernel(
    sizes, scale, a_ref, w_hbm, eb_ref, db_ref, gw_ref, geb_ref, gdb_ref,
    w_ref, raw, xs, prod, sig, lats, grads, res, sr, ss, tl, ts, sr2, ss2, tl2, ts2,
    half_out, half_in, half_own, part_out, part_in, pair_out, pair_in, acc, gacc, gebuf,
    w_sem, h_sem, half_sem, xy_sem, core_sem, line_sem, line2_sem, geb_send, geb_recv,
):
    nf, ny, _, nx, _ = sizes
    nq = ny * nx
    nt, per = 2 * nq, nq // 2
    last = nf - 1
    width, nlat = w_ref.shape[1], w_ref.shape[2]
    f, y, h, x, c = (lax.axis_index(name) for name in AXES)
    q = y * nx + x
    mid = last // 2
    lag = SKEW * jnp.maximum(f, last - f)
    partner, sibling = (f, y, 1 - h, x, c), (f, y, h, x, 1 - c)
    after, before = (jnp.minimum(f + 1, last), y, h, x, c), (jnp.maximum(f - 1, 0), y, h, x, c)
    offsets = [(dy, dx) for dy in range(ny) for dx in range(nx) if dy or dx]
    sent = []

    def at_offset(dy, dx):
        return lax.rem(y + dy + ny, ny), lax.rem(x + dx + nx, nx)

    def remote(src, dst, send, recv, to):
        return pltpu.make_async_remote_copy(
            src_ref=src, dst_ref=dst, send_sem=send, recv_sem=recv,
            device_id=to, device_id_type=pl.DeviceIdType.MESH,
        )

    def start(*args):
        copy = remote(*args)
        copy.start()
        sent.append(copy)
        return copy

    w_copy = pltpu.make_async_copy(w_hbm, w_ref, w_sem)
    w_copy.start()

    barrier = pltpu.get_barrier_semaphore()

    def greet(to):
        pl.semaphore_signal(barrier, inc=1, device_id=to, device_id_type=pl.DeviceIdType.MESH)

    greet(partner)
    for dy, dx in offsets:
        py, px = at_offset(dy, dx)
        greet((f, py, h, px, c))
    greet(sibling)

    @pl.when(f > 0)
    def _():
        greet(before)

    @pl.when(f < last)
    def _():
        greet(after)

    @pl.when(f != mid)
    def _():
        greet((mid, y, h, x, c))

    @pl.when(f == 0)
    def _():
        sr[...] = jnp.zeros_like(sr)
        sr2[...] = jnp.zeros_like(sr2)

    @pl.when(f == last)
    def _():
        tl[...] = jnp.zeros_like(tl)
        tl2[...] = jnp.zeros_like(tl2)

    raw[h, c, q] = a_ref[...]
    gacc[...] = jnp.zeros_like(gacc)

    beside = (f > 0).astype(jnp.int32) + (f < last).astype(jnp.int32)
    listeners = last * (f == mid).astype(jnp.int32)
    pl.semaphore_wait(barrier, 2 + len(offsets) + beside + listeners)

    def spread(src, slot, at):
        for number, (dy, dx) in enumerate(offsets):
            py, px = at_offset(dy, dx)
            start(src, slot(c, q), xy_sem.at[0, at, number], xy_sem.at[1, at, q], (f, py, h, px, c))
        start(src, slot(c, q), core_sem.at[0, at, q], core_sem.at[1, at, q], sibling)

    def collect(slot, at):
        for dy, dx in offsets:
            py, px = at_offset(-dy, -dx)
            source = py * nx + px
            here = slot(c, source)
            remote(here, here, xy_sem.at[0, at, 0], xy_sem.at[1, at, source], sibling).wait_recv()
            start(here, here, core_sem.at[0, at, source], core_sem.at[1, at, source], sibling)

    def settle(slot, at):
        for source in range(nq):
            here = slot(1 - c, source)
            remote(here, here, core_sem.at[0, at, 0], core_sem.at[1, at, source], sibling).wait_recv()

    def products(left, tile, count):
        columns = 256
        tiles = pl.ds(tile, count)

        @pl.loop(0, nlat // columns)
        def _(block):
            cols = pl.ds(pl.multiple_of(block * columns, columns), columns)
            total = jnp.dot(
                left[0, tiles].reshape(count * TILE, width), w_ref[0, :, cols], preferred_element_type=F32
            )
            total = total + jnp.dot(
                left[1, tiles].reshape(count * TILE, width), w_ref[1, :, cols], preferred_element_type=F32
            )
            prod[tiles, :, cols] = total.reshape(count, TILE, columns)

    def chain(bufs, sems, order, on_total):
        right_in, right_out, left_in, left_out = bufs

        def to_right(k):
            return remote(right_out.at[k], right_in.at[k], sems.at[0, k], sems.at[1, k], after)

        def to_left(k):
            return remote(left_out.at[k], left_in.at[k], sems.at[2, k], sems.at[3, k], before)

        def steps(low, high, on_step=None):
            @pl.loop(low, high)
            def _(step):
                right, left, done = step - SKEW * f, step - SKEW * (last - f), step - lag

                @pl.when((right >= 0) & (right < nt))
                def _():
                    k = order(right)

                    @pl.when(f > 0)
                    def _():
                        to_right(k).wait_recv()

                    @pl.when(f < last)
                    def _():
                        right_out[k] = (prod[k] + right_in[k].astype(F32)).astype(BF16)
                        to_right(k).start()

                @pl.when((left >= 0) & (left < nt))
                def _():
                    k = order(left)

                    @pl.when(f < last)
                    def _():
                        to_left(k).wait_recv()

                    @pl.when(f > 0)
                    def _():
                        left_out[k] = (prod[k] + left_in[k].astype(F32)).astype(BF16)
                        to_left(k).start()

                @pl.when((done >= 0) & (done < nt))
                def _():
                    k = order(done)
                    on_total(k, prod[k] + right_in[k].astype(F32) + left_in[k].astype(F32))

                if on_step is not None:
                    on_step(step)

        def drain():
            @pl.loop(0, nt)
            def _(k):
                @pl.when(f < last)
                def _():
                    to_right(k).wait_send()

                @pl.when(f > 0)
                def _():
                    to_left(k).wait_send()

        return steps, drain

    far = 1 - h

    def raw_slot(side):
        return lambda core, source: raw.at[side, core, source]

    def unpack(side):
        rows = TILE // 2

        @pl.loop(0, nq)
        def _(source):
            first, second = raw[side, 0, source].astype(F32), raw[side, 1, source].astype(F32)
            tile = (source // per) * nq + side * per + lax.rem(source, per)
            for m in range(2):
                part = slice(m * rows, (m + 1) * rows)
                xs[m, tile] = jnp.concatenate([first[part], second[part]], axis=0).astype(BF16)

    spread(a_ref, raw_slot(h), 0)
    far_copy = start(a_ref, raw.at[h, c, q], h_sem.at[0, 0], h_sem.at[1, 0], partner)
    collect(raw_slot(h), 0)
    far_here = raw.at[far, c, q]
    remote(far_here, far_here, h_sem.at[0, 0], h_sem.at[1, 0], partner).wait_recv()
    spread(far_here, raw_slot(far), 1)
    settle(raw_slot(h), 0)
    unpack(h)
    w_copy.wait()
    products(xs, h * per, per)

    def activate(k, total):
        pre = total + eb_ref[...]
        fall = jnp.exp(-jnp.abs(pre))
        lats[k] = (jnp.maximum(pre, 0.0) + jnp.log1p(fall)).astype(BF16)
        sig[k] = jnp.where(pre >= 0, 1.0, fall) / (1.0 + fall)

    def own_first(k):
        side = lax.rem(k // per + h, 2)
        return (k // nq) * nq + side * per + lax.rem(k, per)

    steps, drain = chain((sr, ss, tl, ts), line_sem, own_first, activate)
    steps(0, per - 1)
    collect(raw_slot(far), 1)
    steps(per - 1, per)
    settle(raw_slot(far), 1)
    unpack(far)
    products(xs, far * per, per)
    steps(per, per + per // 2)
    products(xs, nq, nq)

    def terms(tile, m):
        return lax.dot_general(
            lats[pl.ds(tile, per)].reshape(per * TILE, nlat), w_ref[m],
            (((1,), (1,)), ((), ())), preferred_element_type=F32,
        ).reshape(per, TILE, width)

    def recon(g):
        for m in range(2):
            half_out[g, m] = terms(g * nq + (1 - c) * per, m).astype(BF16)
        start(half_out.at[g], half_in.at[g], half_sem.at[0, g], half_sem.at[1, g], sibling)
        for m in range(2):
            half_own[g, m] = terms(g * nq + c * per, m)

    def own_part(g, owner):
        m, tile = lax.rem(owner, 2), owner // 2
        return half_own[g, m, tile] + half_in[g, m, tile].astype(F32)

    def scatter(g):
        remote(
            half_out.at[g], half_in.at[g], half_sem.at[0, g], half_sem.at[1, g], sibling
        ).wait_recv()
        for number, (dy, dx) in enumerate(offsets):
            py, px = at_offset(dy, dx)
            part_out[g, number] = own_part(g, py * nx + px).astype(BF16)
            start(
                part_out.at[g, number], part_in.at[g, number],
                xy_sem.at[0, 4 + g, number], xy_sem.at[1, 4 + g, number], (f, py, h, px, c),
            )

    def pair_up(g):
        total = own_part(g, q)
        for number in range(len(offsets)):
            here = part_in.at[g, number]
            remote(here, here, xy_sem.at[0, 4 + g, number], xy_sem.at[1, 4 + g, number], sibling).wait_recv()
            total = total + part_in[g, number].astype(F32)
        pair_out[g] = total.astype(BF16)
        start(pair_out.at[g], pair_in.at[g], h_sem.at[0, 1 + g], h_sem.at[1, 1 + g], partner)

    def res_slot(g):
        return lambda core, source: res.at[lax.rem(source, 2), g * nq + core * per + source // 2]

    def residual(g):
        here = pair_in.at[g]
        remote(here, here, h_sem.at[0, 1 + g], h_sem.at[1, 1 + g], partner).wait_recv()
        m, tile = lax.rem(q, 2), g * nq + c * per + q // 2
        bias = jnp.where(m == 0, db_ref[0:1], db_ref[1:2])
        summed = pair_out[g].astype(F32) + pair_in[g].astype(F32)
        res[m, tile] = (scale * summed + bias - xs[m, tile].astype(F32)).astype(BF16)
        spread(res_slot(g)(c, q), res_slot(g), 2 + g)

    ready = nq + lag
    steps(per + per // 2, ready, None)
    recon(0)
    steps(ready, ready + SCATTER_AT)
    scatter(0)
    steps(ready + SCATTER_AT, ready + PAIR_AT)
    pair_up(0)
    steps(ready + PAIR_AT, nt + lag)
    recon(1)
    scatter(1)
    residual(0)
    pair_up(1)
    collect(res_slot(0), 2)
    settle(res_slot(0), 2)
    products(res, 0, nq)

    channels, columns = 128, 256
    across, along = nlat // columns, width // channels
    blocks = 2 * across * along

    def blocks_of(number):
        chan = pl.ds(pl.multiple_of(lax.rem(number // across, along) * channels, channels), channels)
        cols = pl.ds(pl.multiple_of(lax.rem(number, across) * columns, columns), columns)
        return number // (across * along), chan, cols

    def over_rows(left, m, chan, right, cols, low, count):
        tiles = pl.ds(low, count)
        return lax.dot_general(
            left[m, tiles, :, chan].reshape(count * TILE, channels),
            right[tiles, :, cols].reshape(count * TILE, columns),
            (((0,), (0,)), ((), ())), preferred_element_type=F32,
        )

    def dec_block(number):
        m, chan, cols = blocks_of(number)
        acc[m, chan, cols] = scale * over_rows(res, m, chan, lats, cols, 0, nt)

    def enc_block(number):
        m, chan, cols = blocks_of(number)
        acc[m, chan, cols] += over_rows(xs, m, chan, grads, cols, 0, nq)

    def two_a_step(low, block):
        def on_step(step):
            for number in (2 * (step - low), 2 * (step - low) + 1):
                @pl.when(number < blocks)
                def _():
                    block(number)

        return on_step

    def rest(count, block):
        @pl.loop(jnp.minimum(2 * count, blocks), blocks)
        def _(number):
            block(number)

    def finish(k, total):
        grad = scale * total * sig[k]
        grads[k] = grad.astype(BF16)
        gacc[...] += grad

    steps, drain2 = chain((sr2, ss2, tl2, ts2), line2_sem, lambda k: k, finish)
    steps(0, RESID_AT)
    residual(1)
    steps(RESID_AT, nq - COLLECT_BEFORE)
    collect(res_slot(1), 3)
    steps(nq - COLLECT_BEFORE, nq)
    settle(res_slot(1), 3)
    products(res, nq, nq)
    steps(nq, ready, two_a_step(nq, dec_block))
    rest(lag, dec_block)
    steps(ready, nt + lag, two_a_step(ready, enc_block))
    rest(nq, enc_block)

    def to_chip(ahead):
        return remote(
            gebuf, gebuf, geb_send.at[ahead], geb_recv.at[0], (lax.rem(mid + ahead, nf), y, h, x, c)
        )

    @pl.when(f == mid)
    def _():
        gebuf[...] = jnp.broadcast_to(jnp.sum(gacc[...], axis=0, keepdims=True), gebuf.shape)
        for ahead in range(1, nf):
            to_chip(ahead).start()

    @pl.loop(0, blocks)
    def _(number):
        m, chan, cols = blocks_of(number)
        gw_ref[m, chan, cols] = (acc[m, chan, cols] + over_rows(xs, m, chan, grads, cols, nq, nq)).astype(BF16)

    for m in range(2):
        gdb_ref[m : m + 1] = jnp.sum(jnp.sum(res[m].astype(F32), axis=0), axis=0, keepdims=True)

    drain()
    drain2()
    for copy in sent:
        copy.wait_send()

    @pl.when(f == mid)
    def _():
        for ahead in range(1, nf):
            to_chip(ahead).wait_send()

    @pl.when(f != mid)
    def _():
        to_chip(1).wait_recv()

    geb_ref[...] = gebuf[0:1]


def on_device(sizes, acts, weight, enc_bias, dec_bias):
    nf, ny, nh, nx, nc = sizes
    lat_count = ny * nh * nx * nc
    _, width, nlat = weight.shape
    scale = math.sqrt(2.0 * (width * nf) / (nlat * lat_count))
    nq = ny * nx
    nt, per = 2 * nq, nq // 2
    vmem = pltpu.VMEM
    tiles = vmem((2, nt, TILE, width), BF16)
    chunk = vmem((nt, TILE, nlat), BF16)
    wide = vmem((nt, TILE, nlat), F32)
    half = vmem((2, 2, per, TILE, width), BF16)
    pair = vmem((2, TILE, width), BF16)
    parts = vmem((2, nq - 1, TILE, width), BF16)
    dma = pltpu.SemaphoreType.DMA
    whole = pl.BlockSpec(memory_space=pltpu.VMEM)
    grad_weight, grad_enc, grad_dec = pl.pallas_call(
        functools.partial(chain_kernel, sizes, scale),
        out_shape=(
            jax.ShapeDtypeStruct((2, width, nlat), BF16),
            jax.ShapeDtypeStruct((1, nlat), F32),
            jax.ShapeDtypeStruct((2, width), F32),
        ),
        in_specs=[whole, pl.BlockSpec(memory_space=pl.ANY), whole, whole],
        out_specs=(whole, whole, whole),
        scratch_shapes=[
            vmem((2, width, nlat), BF16), vmem((2, 2, nq, TILE, width), BF16),
            tiles, wide, wide, chunk, chunk, tiles,
            *([chunk] * 8),
            half, half, vmem((2, 2, per, TILE, width), F32), parts, parts, pair, pair,
            vmem((2, width, nlat), F32), vmem((TILE, nlat), F32), vmem((8, nlat), F32),
            dma, dma((2, 3)), dma((2, 2)), dma((2, 6, nq)), dma((2, 4, nq)), dma((4, nt)), dma((4, nt)),
            dma((nf,)), dma((1,)),
        ],
        compiler_params=pltpu.CompilerParams(
            collective_id=0, has_side_effects=True, vmem_limit_bytes=60 * 1024 * 1024
        ),
        name="crosscoder_step",
    )(acts.reshape(TILE, width), weight, enc_bias.reshape(1, nlat), dec_bias)
    return grad_weight, grad_enc.reshape(nlat), grad_dec


def solution(mesh):
    shape = dict(mesh.shape)
    if shape["lat"] == 64:
        sizes = (shape["feat"], 4, 2, 4, 2)
    else:
        sizes = (shape["feat"], 1, 2, shape["lat"] // 4, 2)
    torus = Mesh(mesh.devices.reshape(sizes), AXES)
    in_specs = (P(None, LAT, "feat"), P(None, "feat", LAT), P(LAT), P(None, "feat"))
    out_specs = (P(None, "feat", LAT), P(LAT), P(None, "feat"))
    return jax.shard_map(
        functools.partial(on_device, sizes),
        mesh=torus, in_specs=in_specs, out_specs=out_specs, check_vma=False,
    )
```

```python
import functools
import math

import jax
import jax.numpy as jnp
from jax import lax
from jax.experimental import pallas as pl
from jax.experimental.pallas import tpu as pltpu
from jax.sharding import Mesh
from jax.sharding import PartitionSpec as P

LAT = ("lat_0", "lat_1", "lat_2", "lat_3")
AXES = ("feat", *LAT)
BF16, F32 = jnp.bfloat16, jnp.float32
TILE = 16
SKEW = 9
SCATTER_AT, PAIR_AT = 5, 20
RESID_AT, COLLECT_BEFORE = 10, 4


def chain_kernel(
    sizes, scale, a_ref, w_hbm, eb_ref, db_ref, gw_ref, geb_ref, gdb_ref,
    w_ref, wt, raw, xs, xt, rt, prod, sig, lats, grads, res, sr, ss, tl, ts, sr2, ss2, tl2, ts2,
    half_out, half_in, half_own, part_out, part_in, pair_out, pair_in, acc, gacc, gebuf,
    w_sem, h_sem, half_sem, xy_sem, core_sem, line_sem, line2_sem, geb_send, geb_recv,
):
    nf, ny, _, nx, _ = sizes
    nq = ny * nx
    nt, per = 2 * nq, nq // 2
    last = nf - 1
    width, nlat = w_ref.shape[1], w_ref.shape[2]
    f, y, h, x, c = (lax.axis_index(name) for name in AXES)
    q = y * nx + x
    mid = last // 2
    lag = SKEW * jnp.maximum(f, last - f)
    partner, sibling = (f, y, 1 - h, x, c), (f, y, h, x, 1 - c)
    after, before = (jnp.minimum(f + 1, last), y, h, x, c), (jnp.maximum(f - 1, 0), y, h, x, c)
    offsets = [(dy, dx) for dy in range(ny) for dx in range(nx) if dy or dx]
    sent = []

    def at_offset(dy, dx):
        return lax.rem(y + dy + ny, ny), lax.rem(x + dx + nx, nx)

    def remote(src, dst, send, recv, to):
        return pltpu.make_async_remote_copy(
            src_ref=src, dst_ref=dst, send_sem=send, recv_sem=recv,
            device_id=to, device_id_type=pl.DeviceIdType.MESH,
        )

    def start(*args):
        copy = remote(*args)
        copy.start()
        sent.append(copy)
        return copy

    w_copy = pltpu.make_async_copy(w_hbm, w_ref, w_sem)
    w_copy.start()

    barrier = pltpu.get_barrier_semaphore()

    def greet(to):
        pl.semaphore_signal(barrier, inc=1, device_id=to, device_id_type=pl.DeviceIdType.MESH)

    greet(partner)
    for dy, dx in offsets:
        py, px = at_offset(dy, dx)
        greet((f, py, h, px, c))
    greet(sibling)

    @pl.when(f > 0)
    def _():
        greet(before)

    @pl.when(f < last)
    def _():
        greet(after)

    @pl.when(f != mid)
    def _():
        greet((mid, y, h, x, c))

    @pl.when(f == 0)
    def _():
        sr[...] = jnp.zeros_like(sr)
        sr2[...] = jnp.zeros_like(sr2)

    @pl.when(f == last)
    def _():
        tl[...] = jnp.zeros_like(tl)
        tl2[...] = jnp.zeros_like(tl2)

    raw[h, c, q] = a_ref[...]
    gacc[...] = jnp.zeros_like(gacc)

    beside = (f > 0).astype(jnp.int32) + (f < last).astype(jnp.int32)
    listeners = last * (f == mid).astype(jnp.int32)
    pl.semaphore_wait(barrier, 2 + len(offsets) + beside + listeners)

    def spread(src, slot, at):
        for number, (dy, dx) in enumerate(offsets):
            py, px = at_offset(dy, dx)
            start(src, slot(c, q), xy_sem.at[0, at, number], xy_sem.at[1, at, q], (f, py, h, px, c))
        start(src, slot(c, q), core_sem.at[0, at, q], core_sem.at[1, at, q], sibling)

    def collect(slot, at):
        for dy, dx in offsets:
            py, px = at_offset(-dy, -dx)
            source = py * nx + px
            here = slot(c, source)
            remote(here, here, xy_sem.at[0, at, 0], xy_sem.at[1, at, source], sibling).wait_recv()
            start(here, here, core_sem.at[0, at, source], core_sem.at[1, at, source], sibling)

    def settle(slot, at):
        for source in range(nq):
            here = slot(1 - c, source)
            remote(here, here, core_sem.at[0, at, 0], core_sem.at[1, at, source], sibling).wait_recv()

    def products(left, tile, count):
        tiles = pl.ds(tile, count)
        total = jnp.dot(left[0, tiles].reshape(count * TILE, width), w_ref[0], preferred_element_type=F32)
        total = total + jnp.dot(left[1, tiles].reshape(count * TILE, width), w_ref[1], preferred_element_type=F32)
        prod[tiles] = total.reshape(count, TILE, nlat)

    def turned(left, right):
        for m in range(2):
            right[m] = left[m].reshape(nt * TILE, width).T

    piece = nlat // 2
    pieces = 2 * nt

    def half_of(k):
        return pl.ds(pl.multiple_of(lax.rem(k, 2) * piece, piece), piece)

    def chain(bufs, sems, order, on_total):
        right_in, right_out, left_in, left_out = bufs

        def to_right(k):
            return remote(right_out.at[k], right_in.at[k], sems.at[0, k], sems.at[1, k], after)

        def to_left(k):
            return remote(left_out.at[k], left_in.at[k], sems.at[2, k], sems.at[3, k], before)

        def steps(low, high, on_step=None):
            @pl.loop(low, high)
            def _(step):
                right, left, done = step - SKEW * f, step - SKEW * (last - f), step - lag

                @pl.when((right >= 0) & (right < pieces))
                def _():
                    tile, k, cols = order(right)

                    @pl.when(f > 0)
                    def _():
                        to_right(k).wait_recv()

                    @pl.when(f < last)
                    def _():
                        right_out[k] = (prod[tile, :, cols] + right_in[k].astype(F32)).astype(BF16)
                        to_right(k).start()

                @pl.when((left >= 0) & (left < pieces))
                def _():
                    tile, k, cols = order(left)

                    @pl.when(f < last)
                    def _():
                        to_left(k).wait_recv()

                    @pl.when(f > 0)
                    def _():
                        left_out[k] = (prod[tile, :, cols] + left_in[k].astype(F32)).astype(BF16)
                        to_left(k).start()

                @pl.when((done >= 0) & (done < pieces))
                def _():
                    tile, k, cols = order(done)
                    on_total(tile, cols, prod[tile, :, cols] + right_in[k].astype(F32) + left_in[k].astype(F32))

                if on_step is not None:
                    on_step(step)

        def drain():
            @pl.loop(0, pieces)
            def _(k):
                @pl.when(f < last)
                def _():
                    to_right(k).wait_send()

                @pl.when(f > 0)
                def _():
                    to_left(k).wait_send()

        return steps, drain

    far = 1 - h

    def raw_slot(side):
        return lambda core, source: raw.at[side, core, source]

    def unpack(side):
        rows = TILE // 2

        @pl.loop(0, nq)
        def _(source):
            first, second = raw[side, 0, source].astype(F32), raw[side, 1, source].astype(F32)
            tile = (source // per) * nq + side * per + lax.rem(source, per)
            for m in range(2):
                part = slice(m * rows, (m + 1) * rows)
                xs[m, tile] = jnp.concatenate([first[part], second[part]], axis=0).astype(BF16)

    start(a_ref, raw.at[h, c, q], h_sem.at[0, 0], h_sem.at[1, 0], partner)
    spread(a_ref, raw_slot(h), 0)
    w_copy.wait()
    for m in range(2):
        wt[m] = w_ref[m].T
    collect(raw_slot(h), 0)
    far_here = raw.at[far, c, q]
    remote(far_here, far_here, h_sem.at[0, 0], h_sem.at[1, 0], partner).wait_recv()
    spread(far_here, raw_slot(far), 1)
    settle(raw_slot(h), 0)
    unpack(h)
    products(xs, h * per, per)

    def activate(k, cols, total):
        pre = total + eb_ref[:, cols]
        fall = jnp.exp(-jnp.abs(pre))
        lats[k, :, cols] = (jnp.maximum(pre, 0.0) + jnp.log1p(fall)).astype(BF16)
        sig[k, :, cols] = jnp.where(pre >= 0, 1.0, fall) / (1.0 + fall)

    def own_first(number):
        k = number // 2
        side = lax.rem(k // per + h, 2)
        tile = (k // nq) * nq + side * per + lax.rem(k, per)
        return tile, 2 * tile + lax.rem(number, 2), half_of(number)

    steps, drain = chain((sr, ss, tl, ts), line_sem, own_first, activate)
    steps(0, nq - 2)
    collect(raw_slot(far), 1)
    steps(nq - 2, nq)
    settle(raw_slot(far), 1)
    unpack(far)
    products(xs, far * per, per)
    steps(nq, nq + per)
    products(xs, nq, nq)

    def terms(tile, m):
        return lax.dot_general(
            lats[pl.ds(tile, per)].reshape(per * TILE, nlat), wt[m],
            (((1,), (0,)), ((), ())), preferred_element_type=F32,
        ).reshape(per, TILE, width)

    def recon(g):
        for m in range(2):
            half_out[g, m] = terms(g * nq + (1 - c) * per, m).astype(BF16)
        start(half_out.at[g], half_in.at[g], half_sem.at[0, g], half_sem.at[1, g], sibling)
        for m in range(2):
            half_own[g, m] = terms(g * nq + c * per, m)

    def own_part(g, owner):
        m, tile = lax.rem(owner, 2), owner // 2
        return half_own[g, m, tile] + half_in[g, m, tile].astype(F32)

    def scatter(g):
        remote(
            half_out.at[g], half_in.at[g], half_sem.at[0, g], half_sem.at[1, g], sibling
        ).wait_recv()
        for number, (dy, dx) in enumerate(offsets):
            py, px = at_offset(dy, dx)
            part_out[g, number] = own_part(g, py * nx + px).astype(BF16)
            start(
                part_out.at[g, number], part_in.at[g, number],
                xy_sem.at[0, 4 + g, number], xy_sem.at[1, 4 + g, number], (f, py, h, px, c),
            )

    def pair_up(g):
        total = own_part(g, q)
        for number in range(len(offsets)):
            here = part_in.at[g, number]
            remote(here, here, xy_sem.at[0, 4 + g, number], xy_sem.at[1, 4 + g, number], sibling).wait_recv()
            total = total + part_in[g, number].astype(F32)
        pair_out[g] = total.astype(BF16)
        start(pair_out.at[g], pair_in.at[g], h_sem.at[0, 1 + g], h_sem.at[1, 1 + g], partner)

    def res_slot(g):
        return lambda core, source: res.at[lax.rem(source, 2), g * nq + core * per + source // 2]

    def residual(g):
        here = pair_in.at[g]
        remote(here, here, h_sem.at[0, 1 + g], h_sem.at[1, 1 + g], partner).wait_recv()
        m, tile = lax.rem(q, 2), g * nq + c * per + q // 2
        bias = jnp.where(m == 0, db_ref[0:1], db_ref[1:2])
        summed = pair_out[g].astype(F32) + pair_in[g].astype(F32)
        res[m, tile] = (scale * summed + bias - xs[m, tile].astype(F32)).astype(BF16)
        spread(res_slot(g)(c, q), res_slot(g), 2 + g)

    ready = nt + lag
    steps(nq + per, ready)
    recon(0)
    steps(ready, ready + SCATTER_AT)
    scatter(0)
    steps(ready + SCATTER_AT, ready + PAIR_AT)
    pair_up(0)
    steps(ready + PAIR_AT, pieces + lag)
    recon(1)
    scatter(1)
    residual(0)
    turned(xs, xt)
    pair_up(1)
    collect(res_slot(0), 2)
    settle(res_slot(0), 2)
    products(res, 0, nq)

    below = nq * TILE

    def dec_block(number):
        m, cols = number // 2, half_of(number)
        acc[m, :, cols] = scale * jnp.dot(
            rt[m], lats[:, :, cols].reshape(nt * TILE, piece), preferred_element_type=F32
        )

    def enc_block(number):
        m, cols = number // 2, half_of(number)
        acc[m, :, cols] += jnp.dot(
            xt[m, :, :below], grads[:nq, :, cols].reshape(below, piece), preferred_element_type=F32
        )

    def blocks_from(low, block):
        def on_step(step):
            @pl.when(step - low < 4)
            def _():
                block(step - low)

        return on_step

    def finish(k, cols, total):
        grad = scale * total * sig[k, :, cols]
        grads[k, :, cols] = grad.astype(BF16)
        gacc[:, cols] += grad

    steps, drain2 = chain(
        (sr2, ss2, tl2, ts2), line2_sem, lambda number: (number // 2, number, half_of(number)), finish
    )
    steps(0, RESID_AT)
    residual(1)
    steps(RESID_AT, nt - COLLECT_BEFORE)
    collect(res_slot(1), 3)
    steps(nt - COLLECT_BEFORE, nt)
    settle(res_slot(1), 3)
    products(res, nq, nq)
    turned(res, rt)
    for m in range(2):
        gdb_ref[m : m + 1] = jnp.sum(jnp.sum(res[m].astype(F32), axis=0), axis=0, keepdims=True)
    steps(nt, ready, blocks_from(nt, dec_block))
    steps(ready, pieces + lag, blocks_from(ready, enc_block))

    def to_chip(ahead):
        return remote(
            gebuf, gebuf, geb_send.at[ahead], geb_recv.at[0], (lax.rem(mid + ahead, nf), y, h, x, c)
        )

    @pl.when(f == mid)
    def _():
        gebuf[...] = jnp.broadcast_to(jnp.sum(gacc[...], axis=0, keepdims=True), gebuf.shape)
        for ahead in range(1, nf):
            to_chip(ahead).start()

    for m in range(2):
        rest = jnp.dot(xt[m, :, below:], grads[nq:].reshape(below, nlat), preferred_element_type=F32)
        gw_ref[m] = (acc[m] + rest).astype(BF16)

    drain()
    drain2()
    for copy in sent:
        copy.wait_send()

    @pl.when(f == mid)
    def _():
        for ahead in range(1, nf):
            to_chip(ahead).wait_send()

    @pl.when(f != mid)
    def _():
        to_chip(1).wait_recv()

    geb_ref[...] = gebuf[0:1]


def on_device(sizes, acts, weight, enc_bias, dec_bias):
    nf, ny, nh, nx, nc = sizes
    lat_count = ny * nh * nx * nc
    _, width, nlat = weight.shape
    scale = math.sqrt(2.0 * (width * nf) / (nlat * lat_count))
    nq = ny * nx
    nt, per = 2 * nq, nq // 2
    vmem = pltpu.VMEM
    tiles = vmem((2, nt, TILE, width), BF16)
    chunk = vmem((nt, TILE, nlat), BF16)
    wide = vmem((nt, TILE, nlat), F32)
    flow = vmem((2 * nt, TILE, nlat // 2), BF16)
    turned = vmem((2, width, nt * TILE), BF16)
    half = vmem((2, 2, per, TILE, width), BF16)
    pair = vmem((2, TILE, width), BF16)
    parts = vmem((2, nq - 1, TILE, width), BF16)
    dma = pltpu.SemaphoreType.DMA
    whole = pl.BlockSpec(memory_space=pltpu.VMEM)
    grad_weight, grad_enc, grad_dec = pl.pallas_call(
        functools.partial(chain_kernel, sizes, scale),
        out_shape=(
            jax.ShapeDtypeStruct((2, width, nlat), BF16),
            jax.ShapeDtypeStruct((1, nlat), F32),
            jax.ShapeDtypeStruct((2, width), F32),
        ),
        in_specs=[whole, pl.BlockSpec(memory_space=pl.ANY), whole, whole],
        out_specs=(whole, whole, whole),
        scratch_shapes=[
            vmem((2, width, nlat), BF16), vmem((2, nlat, width), BF16), vmem((2, 2, nq, TILE, width), BF16),
            tiles, turned, turned, wide, wide, chunk, chunk, tiles,
            *([flow] * 8),
            half, half, vmem((2, 2, per, TILE, width), F32), parts, parts, pair, pair,
            vmem((2, width, nlat), F32), vmem((TILE, nlat), F32), vmem((8, nlat), F32),
            dma, dma((2, 3)), dma((2, 2)), dma((2, 6, nq)), dma((2, 4, nq)), dma((4, 2 * nt)), dma((4, 2 * nt)),
            dma((nf,)), dma((1,)),
        ],
        compiler_params=pltpu.CompilerParams(
            collective_id=0, has_side_effects=True, vmem_limit_bytes=60 * 1024 * 1024
        ),
        name="crosscoder_step",
    )(acts.reshape(TILE, width), weight, enc_bias.reshape(1, nlat), dec_bias)
    return grad_weight, grad_enc.reshape(nlat), grad_dec


def solution(mesh):
    shape = dict(mesh.shape)
    if shape["lat"] == 64:
        sizes = (shape["feat"], 4, 2, 4, 2)
    else:
        sizes = (shape["feat"], 1, 2, shape["lat"] // 4, 2)
    torus = Mesh(mesh.devices.reshape(sizes), AXES)
    in_specs = (P(None, LAT, "feat"), P(None, "feat", LAT), P(LAT), P(None, "feat"))
    out_specs = (P(None, "feat", LAT), P(LAT), P(None, "feat"))
    return jax.shard_map(
        functools.partial(on_device, sizes),
        mesh=torus, in_specs=in_specs, out_specs=out_specs, check_vma=False,
    )
```

```python
import functools
import math

import jax
import jax.numpy as jnp
from jax import lax
from jax.experimental import pallas as pl
from jax.experimental.pallas import tpu as pltpu
from jax.sharding import Mesh
from jax.sharding import PartitionSpec as P

LAT = ("lat_0", "lat_1", "lat_2", "lat_3")
AXES = ("feat", *LAT)
BF16, F32 = jnp.bfloat16, jnp.float32
TILE = 16
SKEW = 9
GROUPS = 4


def chain_kernel(
    sizes, scale, a_ref, w_hbm, eb_ref, db_ref, gw_ref, geb_ref, gdb_ref,
    w_ref, wt, raw, xs, xt, rt, prod, sig, lats, grads, res, sr, ss, tl, ts, sr2, ss2, tl2, ts2,
    half_out, half_in, half_own, part_out, part_in, pair_out, pair_in, acc, gacc, gebuf,
    w_sem, h_sem, half_sem, xy_sem, core_sem, line_sem, line2_sem, geb_send, geb_recv,
):
    nf, ny, _, nx, _ = sizes
    nq = ny * nx
    nt, per = 2 * nq, nq // GROUPS
    split = GROUPS // 2
    last = nf - 1
    width, nlat = w_ref.shape[1], w_ref.shape[2]
    f, y, h, x, c = (lax.axis_index(name) for name in AXES)
    q = y * nx + x
    mid = last // 2
    lag = SKEW * jnp.maximum(f, last - f)
    partner, sibling = (f, y, 1 - h, x, c), (f, y, h, x, 1 - c)
    after, before = (jnp.minimum(f + 1, last), y, h, x, c), (jnp.maximum(f - 1, 0), y, h, x, c)
    offsets = [(dy, dx) for dy in range(ny) for dx in range(nx) if dy or dx]
    sent = []

    def at_offset(dy, dx):
        return lax.rem(y + dy + ny, ny), lax.rem(x + dx + nx, nx)

    def remote(src, dst, send, recv, to):
        return pltpu.make_async_remote_copy(
            src_ref=src, dst_ref=dst, send_sem=send, recv_sem=recv,
            device_id=to, device_id_type=pl.DeviceIdType.MESH,
        )

    def start(*args):
        copy = remote(*args)
        copy.start()
        sent.append(copy)
        return copy

    w_copy = pltpu.make_async_copy(w_hbm, w_ref, w_sem)
    w_copy.start()

    barrier = pltpu.get_barrier_semaphore()

    def greet(to):
        pl.semaphore_signal(barrier, inc=1, device_id=to, device_id_type=pl.DeviceIdType.MESH)

    greet(partner)
    for dy, dx in offsets:
        py, px = at_offset(dy, dx)
        greet((f, py, h, px, c))
    greet(sibling)

    @pl.when(f > 0)
    def _():
        greet(before)

    @pl.when(f < last)
    def _():
        greet(after)

    @pl.when(f != mid)
    def _():
        greet((mid, y, h, x, c))

    @pl.when(f == 0)
    def _():
        sr[...] = jnp.zeros_like(sr)
        sr2[...] = jnp.zeros_like(sr2)

    @pl.when(f == last)
    def _():
        tl[...] = jnp.zeros_like(tl)
        tl2[...] = jnp.zeros_like(tl2)

    raw[h, c, q] = a_ref[...]
    gacc[...] = jnp.zeros_like(gacc)

    beside = (f > 0).astype(jnp.int32) + (f < last).astype(jnp.int32)
    listeners = last * (f == mid).astype(jnp.int32)
    pl.semaphore_wait(barrier, 2 + len(offsets) + beside + listeners)

    def spread(src, slot, at):
        for number, (dy, dx) in enumerate(offsets):
            py, px = at_offset(dy, dx)
            start(src, slot(c, q), xy_sem.at[0, at, number], xy_sem.at[1, at, q], (f, py, h, px, c))
        start(src, slot(c, q), core_sem.at[0, at, q], core_sem.at[1, at, q], sibling)

    def collect(slot, at):
        for dy, dx in offsets:
            py, px = at_offset(-dy, -dx)
            source = py * nx + px
            here = slot(c, source)
            remote(here, here, xy_sem.at[0, at, 0], xy_sem.at[1, at, source], sibling).wait_recv()
            start(here, here, core_sem.at[0, at, source], core_sem.at[1, at, source], sibling)

    def settle(slot, at):
        for source in range(nq):
            here = slot(1 - c, source)
            remote(here, here, core_sem.at[0, at, 0], core_sem.at[1, at, source], sibling).wait_recv()

    def products(left, count, *tiles):
        rows = count * TILE

        def of_model(m):
            parts = [left[m, pl.ds(tile, count)].reshape(rows, width) for tile in tiles]
            return jnp.dot(jnp.concatenate(parts, axis=0), w_ref[m], preferred_element_type=F32)

        total = of_model(0) + of_model(1)
        for number, tile in enumerate(tiles):
            prod[pl.ds(tile, count)] = total[number * rows : (number + 1) * rows].reshape(count, TILE, nlat)

    def turned(left, right):
        for m in range(2):
            right[m] = left[m].reshape(nt * TILE, width).T

    piece = nlat // 2
    pieces = 2 * nt

    def half_of(k):
        return pl.ds(pl.multiple_of(lax.rem(k, 2) * piece, piece), piece)

    def chain(bufs, sems, order, on_total):
        right_in, right_out, left_in, left_out = bufs

        def to_right(k):
            return remote(right_out.at[k], right_in.at[k], sems.at[0, k], sems.at[1, k], after)

        def to_left(k):
            return remote(left_out.at[k], left_in.at[k], sems.at[2, k], sems.at[3, k], before)

        def steps(low, high, on_step=None):
            @pl.loop(low, high)
            def _(step):
                right, left, done = step - SKEW * f, step - SKEW * (last - f), step - lag

                @pl.when((right >= 0) & (right < pieces))
                def _():
                    tile, k, cols = order(right)

                    @pl.when(f > 0)
                    def _():
                        to_right(k).wait_recv()

                    @pl.when(f < last)
                    def _():
                        right_out[k] = (prod[tile, :, cols] + right_in[k].astype(F32)).astype(BF16)
                        to_right(k).start()

                @pl.when((left >= 0) & (left < pieces))
                def _():
                    tile, k, cols = order(left)

                    @pl.when(f < last)
                    def _():
                        to_left(k).wait_recv()

                    @pl.when(f > 0)
                    def _():
                        left_out[k] = (prod[tile, :, cols] + left_in[k].astype(F32)).astype(BF16)
                        to_left(k).start()

                @pl.when((done >= 0) & (done < pieces))
                def _():
                    tile, k, cols = order(done)
                    on_total(tile, cols, prod[tile, :, cols] + right_in[k].astype(F32) + left_in[k].astype(F32))

                if on_step is not None:
                    on_step(step)

        def drain():
            @pl.loop(0, pieces)
            def _(k):
                @pl.when(f < last)
                def _():
                    to_right(k).wait_send()

                @pl.when(f > 0)
                def _():
                    to_left(k).wait_send()

        return steps, drain

    far = 1 - h

    def raw_slot(side):
        return lambda core, source: raw.at[side, core, source]

    def unpack(side):
        rows = TILE // 2

        @pl.loop(0, nq)
        def _(source):
            first, second = raw[side, 0, source].astype(F32), raw[side, 1, source].astype(F32)
            tile = (source // per) * 2 * per + side * per + lax.rem(source, per)
            for m in range(2):
                part = slice(m * rows, (m + 1) * rows)
                xs[m, tile] = jnp.concatenate([first[part], second[part]], axis=0).astype(BF16)

    start(a_ref, raw.at[h, c, q], h_sem.at[0, 0], h_sem.at[1, 0], partner)
    spread(a_ref, raw_slot(h), 0)
    w_copy.wait()
    for m in range(2):
        wt[m] = w_ref[m].T
    collect(raw_slot(h), 0)
    far_here = raw.at[far, c, q]
    remote(far_here, far_here, h_sem.at[0, 0], h_sem.at[1, 0], partner).wait_recv()
    spread(far_here, raw_slot(far), 1)
    settle(raw_slot(h), 0)
    unpack(h)
    products(xs, per, h * per, (2 + h) * per)

    def activate(k, cols, total):
        pre = total + eb_ref[:, cols]
        fall = jnp.exp(-jnp.abs(pre))
        lats[k, :, cols] = (jnp.maximum(pre, 0.0) + jnp.log1p(fall)).astype(BF16)
        sig[k, :, cols] = jnp.where(pre >= 0, 1.0, fall) / (1.0 + fall)

    def own_first(number):
        k = number // 2
        late, turn = k // (4 * per), lax.rem(k // per, 4)
        side = jnp.where(late == 0, turn // 2, lax.rem(turn, 2))
        group = jnp.where(late == 0, lax.rem(turn, 2), turn // 2 + 2 * late)
        tile = group * 2 * per + lax.rem(side + h, 2) * per + lax.rem(k, per)
        return tile, 2 * tile + lax.rem(number, 2), half_of(number)

    steps, drain = chain((sr, ss, tl, ts), line_sem, own_first, activate)
    steps(0, nq - 2)
    collect(raw_slot(far), 1)
    steps(nq - 2, nq)
    settle(raw_slot(far), 1)
    unpack(far)
    products(xs, per, far * per, (2 + far) * per)
    steps(nq, nq + nq // 4)
    products(xs, nq, nq)

    def terms(tile, m):
        return lax.dot_general(
            lats[pl.ds(tile, per)].reshape(per * TILE, nlat), wt[m],
            (((1,), (0,)), ((), ())), preferred_element_type=F32,
        ).reshape(per, TILE, width)

    def recon(g):
        for m in range(2):
            half_out[g, m] = terms((2 * g + 1 - c) * per, m).astype(BF16)
        start(half_out.at[g], half_in.at[g], half_sem.at[0, g], half_sem.at[1, g], sibling)
        for m in range(2):
            half_own[g, m] = terms((2 * g + c) * per, m)

    part_width = width // split

    def block_of(owner):
        first = pl.multiple_of(lax.rem(owner, split) * part_width, part_width)
        return lax.rem(owner // split, 2), owner // (2 * split), pl.ds(first, part_width)

    def own_part(g, owner):
        m, tile, chan = block_of(owner)
        return half_own[g, m, tile, :, chan] + half_in[g, m, tile, :, chan].astype(F32)

    def scatter(g):
        remote(
            half_out.at[g], half_in.at[g], half_sem.at[0, g], half_sem.at[1, g], sibling
        ).wait_recv()
        for number, (dy, dx) in enumerate(offsets):
            py, px = at_offset(dy, dx)
            part_out[g, number] = own_part(g, py * nx + px).astype(BF16)
            start(
                part_out.at[g, number], part_in.at[g, number],
                xy_sem.at[0, 2 + GROUPS + g, number], xy_sem.at[1, 2 + GROUPS + g, number], (f, py, h, px, c),
            )

    def pair_up(g):
        total = own_part(g, q)
        for number in range(len(offsets)):
            here = part_in.at[g, number]
            remote(here, here, xy_sem.at[0, 2 + GROUPS + g, number], xy_sem.at[1, 2 + GROUPS + g, number], sibling).wait_recv()
            total = total + part_in[g, number].astype(F32)
        pair_out[g] = total.astype(BF16)
        start(pair_out.at[g], pair_in.at[g], h_sem.at[0, 1 + g], h_sem.at[1, 1 + g], partner)

    def res_slot(g):
        def slot(core, source):
            m, tile, chan = block_of(source)
            return res.at[m, (2 * g + core) * per + tile, :, chan]

        return slot

    def residual(g):
        here = pair_in.at[g]
        remote(here, here, h_sem.at[0, 1 + g], h_sem.at[1, 1 + g], partner).wait_recv()
        m, tile, chan = block_of(q)
        tile = (2 * g + c) * per + tile
        bias = jnp.where(m == 0, db_ref[0:1, chan], db_ref[1:2, chan])
        summed = pair_out[g].astype(F32) + pair_in[g].astype(F32)
        res[m, tile, :, chan] = (scale * summed + bias - xs[m, tile, :, chan].astype(F32)).astype(BF16)
        spread(res_slot(g)(c, q), res_slot(g), 2 + g)

    def gather(g):
        collect(res_slot(g), 2 + g)

    def arrived(g):
        settle(res_slot(g), 2 + g)
        products(res, 2 * per, 2 * g * per)

    def run(low, base, plan, high):
        for at, stage, g in plan:
            steps(low, base + at)
            stage(g)
            low = base + at
        steps(low, high)

    ready = nt + lag
    first = 6 * per
    run(nq + nq // 4, lag, [
        (first, recon, 0), (first + nq // 4, scatter, 0), (8 * per, recon, 1), (8 * per + nq // 4, scatter, 1),
        (10 * per + nq // 8, pair_up, 0), (12 * per, recon, 2), (12 * per + nq // 8, pair_up, 1),
        (13 * per, scatter, 2), (15 * per + nq // 8, residual, 0),
    ], pieces + lag)
    recon(3)
    pair_up(2)
    scatter(3)
    residual(1)
    turned(xs, xt)
    gather(0)
    arrived(0)

    below = nq * TILE

    def dec_block(number):
        m, cols = number // 2, half_of(number)
        acc[m, :, cols] = scale * jnp.dot(
            rt[m], lats[:, :, cols].reshape(nt * TILE, piece), preferred_element_type=F32
        )

    def enc_block(number):
        m, cols = number // 2, half_of(number)
        acc[m, :, cols] += jnp.dot(
            xt[m, :, :below], grads[:nq, :, cols].reshape(below, piece), preferred_element_type=F32
        )

    def blocks_from(low, block):
        def on_step(step):
            @pl.when(step - low < 4)
            def _():
                block(step - low)

        return on_step

    def finish(k, cols, total):
        grad = scale * total * sig[k, :, cols]
        grads[k, :, cols] = grad.astype(BF16)
        gacc[:, cols] += grad

    steps, drain2 = chain(
        (sr2, ss2, tl2, ts2), line2_sem, lambda number: (number // 2, number, half_of(number)), finish
    )
    run(0, 0, [
        (nq // 8, pair_up, 3), (nq // 4 + nq // 8, gather, 1), (nq // 4 + nq // 8, residual, 2), (2 * per, arrived, 1),
        (5 * per + nq // 8, gather, 2), (5 * per + nq // 8, residual, 3), (6 * per, arrived, 2),
        (9 * per + nq // 8, gather, 3), (10 * per, arrived, 3),
    ], 10 * per)
    turned(res, rt)
    for m in range(2):
        gdb_ref[m : m + 1] = jnp.sum(jnp.sum(res[m].astype(F32), axis=0), axis=0, keepdims=True)
    steps(10 * per, ready, blocks_from(10 * per, dec_block))
    steps(ready, pieces + lag, blocks_from(ready, enc_block))

    def to_chip(ahead):
        return remote(
            gebuf, gebuf, geb_send.at[ahead], geb_recv.at[0], (lax.rem(mid + ahead, nf), y, h, x, c)
        )

    @pl.when(f == mid)
    def _():
        gebuf[...] = jnp.broadcast_to(jnp.sum(gacc[...], axis=0, keepdims=True), gebuf.shape)
        for ahead in range(1, nf):
            to_chip(ahead).start()

    for m in range(2):
        rest = jnp.dot(xt[m, :, below:], grads[nq:].reshape(below, nlat), preferred_element_type=F32)
        gw_ref[m] = (acc[m] + rest).astype(BF16)

    drain()
    drain2()
    for copy in sent:
        copy.wait_send()

    @pl.when(f == mid)
    def _():
        for ahead in range(1, nf):
            to_chip(ahead).wait_send()

    @pl.when(f != mid)
    def _():
        to_chip(1).wait_recv()

    geb_ref[...] = gebuf[0:1]


def on_device(sizes, acts, weight, enc_bias, dec_bias):
    nf, ny, nh, nx, nc = sizes
    lat_count = ny * nh * nx * nc
    _, width, nlat = weight.shape
    scale = math.sqrt(2.0 * (width * nf) / (nlat * lat_count))
    nq = ny * nx
    nt, per = 2 * nq, nq // GROUPS
    vmem = pltpu.VMEM
    tiles = vmem((2, nt, TILE, width), BF16)
    chunk = vmem((nt, TILE, nlat), BF16)
    wide = vmem((nt, TILE, nlat), F32)
    flow = vmem((2 * nt, TILE, nlat // 2), BF16)
    turned = vmem((2, width, nt * TILE), BF16)
    half = vmem((GROUPS, 2, per, TILE, width), BF16)
    pair = vmem((GROUPS, TILE, 2 * width // GROUPS), BF16)
    parts = vmem((GROUPS, nq - 1, TILE, 2 * width // GROUPS), BF16)
    dma = pltpu.SemaphoreType.DMA
    whole = pl.BlockSpec(memory_space=pltpu.VMEM)
    grad_weight, grad_enc, grad_dec = pl.pallas_call(
        functools.partial(chain_kernel, sizes, scale),
        out_shape=(
            jax.ShapeDtypeStruct((2, width, nlat), BF16),
            jax.ShapeDtypeStruct((1, nlat), F32),
            jax.ShapeDtypeStruct((2, width), F32),
        ),
        in_specs=[whole, pl.BlockSpec(memory_space=pl.ANY), whole, whole],
        out_specs=(whole, whole, whole),
        scratch_shapes=[
            vmem((2, width, nlat), BF16), vmem((2, nlat, width), BF16), vmem((2, 2, nq, TILE, width), BF16),
            tiles, turned, turned, wide, wide, chunk, chunk, tiles,
            *([flow] * 8),
            half, half, vmem((GROUPS, 2, per, TILE, width), F32), parts, parts, pair, pair,
            vmem((2, width, nlat), F32), vmem((TILE, nlat), F32), vmem((8, nlat), F32),
            dma, dma((2, 1 + GROUPS)), dma((2, GROUPS)), dma((2, 2 + 2 * GROUPS, nq)), dma((2, 2 + GROUPS, nq)), dma((4, 2 * nt)), dma((4, 2 * nt)),
            dma((nf,)), dma((1,)),
        ],
        compiler_params=pltpu.CompilerParams(
            collective_id=0, has_side_effects=True, vmem_limit_bytes=60 * 1024 * 1024
        ),
        name="crosscoder_step",
    )(acts.reshape(TILE, width), weight, enc_bias.reshape(1, nlat), dec_bias)
    return grad_weight, grad_enc.reshape(nlat), grad_dec


def solution(mesh):
    shape = dict(mesh.shape)
    if shape["lat"] == 64:
        sizes = (shape["feat"], 4, 2, 4, 2)
    else:
        sizes = (shape["feat"], 1, 2, shape["lat"] // 4, 2)
    torus = Mesh(mesh.devices.reshape(sizes), AXES)
    in_specs = (P(None, LAT, "feat"), P(None, "feat", LAT), P(LAT), P(None, "feat"))
    out_specs = (P(None, "feat", LAT), P(LAT), P(None, "feat"))
    return jax.shard_map(
        functools.partial(on_device, sizes),
        mesh=torus, in_specs=in_specs, out_specs=out_specs, check_vma=False,
    )
```

```python
import functools
import math

import jax
import jax.numpy as jnp
from jax import lax
from jax.experimental import pallas as pl
from jax.experimental.pallas import tpu as pltpu
from jax.sharding import Mesh
from jax.sharding import PartitionSpec as P

LAT = ("lat_0", "lat_1", "lat_2", "lat_3")
AXES = ("feat", *LAT)
BF16, F32 = jnp.bfloat16, jnp.float32
TILE = 16
SKEW = 9
GROUPS = 4


def chain_kernel(
    sizes, scale, a_ref, w_hbm, eb_ref, db_ref, acc_out, xt_out, grads_out, geb_ref, gdb_ref,
    w_ref, wt, raw, xs, xt, rt, prod, sig, lats, grads, res, sr, ss, tl, ts, sr2, ss2, tl2, ts2,
    half_out, half_in, half_own, part_out, part_in, pair_out, pair_in, acc, gacc, gebuf,
    w_sem, h_sem, half_sem, xy_sem, core_sem, line_sem, line2_sem, geb_send, geb_recv, out_sem,
):
    nf, ny, _, nx, _ = sizes
    nq = ny * nx
    nt, per = 2 * nq, nq // GROUPS
    split = GROUPS // 2
    last = nf - 1
    width, nlat = w_ref.shape[1], w_ref.shape[2]
    f, y, h, x, c = (lax.axis_index(name) for name in AXES)
    q = y * nx + x
    mid = last // 2
    lag = SKEW * jnp.maximum(f, last - f)
    partner, sibling = (f, y, 1 - h, x, c), (f, y, h, x, 1 - c)
    after, before = (jnp.minimum(f + 1, last), y, h, x, c), (jnp.maximum(f - 1, 0), y, h, x, c)
    offsets = [(dy, dx) for dy in range(ny) for dx in range(nx) if dy or dx]
    sent = []

    def at_offset(dy, dx):
        return lax.rem(y + dy + ny, ny), lax.rem(x + dx + nx, nx)

    def remote(src, dst, send, recv, to):
        return pltpu.make_async_remote_copy(
            src_ref=src, dst_ref=dst, send_sem=send, recv_sem=recv,
            device_id=to, device_id_type=pl.DeviceIdType.MESH,
        )

    def start(*args):
        copy = remote(*args)
        copy.start()
        sent.append(copy)
        return copy

    w_copy = pltpu.make_async_copy(w_hbm, w_ref, w_sem)
    w_copy.start()

    barrier = pltpu.get_barrier_semaphore()

    def greet(to):
        pl.semaphore_signal(barrier, inc=1, device_id=to, device_id_type=pl.DeviceIdType.MESH)

    greet(partner)
    for dy, dx in offsets:
        py, px = at_offset(dy, dx)
        greet((f, py, h, px, c))
    greet(sibling)

    @pl.when(f > 0)
    def _():
        greet(before)

    @pl.when(f < last)
    def _():
        greet(after)

    @pl.when(f != mid)
    def _():
        greet((mid, y, h, x, c))

    @pl.when(f == 0)
    def _():
        sr[...] = jnp.zeros_like(sr)
        sr2[...] = jnp.zeros_like(sr2)

    @pl.when(f == last)
    def _():
        tl[...] = jnp.zeros_like(tl)
        tl2[...] = jnp.zeros_like(tl2)

    raw[h, c, q] = a_ref[...]
    gacc[...] = jnp.zeros_like(gacc)

    beside = (f > 0).astype(jnp.int32) + (f < last).astype(jnp.int32)
    listeners = last * (f == mid).astype(jnp.int32)
    pl.semaphore_wait(barrier, 2 + len(offsets) + beside + listeners)

    def spread(src, slot, at):
        for number, (dy, dx) in enumerate(offsets):
            py, px = at_offset(dy, dx)
            start(src, slot(c, q), xy_sem.at[0, at, number], xy_sem.at[1, at, q], (f, py, h, px, c))
        start(src, slot(c, q), core_sem.at[0, at, q], core_sem.at[1, at, q], sibling)

    def collect(slot, at):
        for dy, dx in offsets:
            py, px = at_offset(-dy, -dx)
            source = py * nx + px
            here = slot(c, source)
            remote(here, here, xy_sem.at[0, at, 0], xy_sem.at[1, at, source], sibling).wait_recv()
            start(here, here, core_sem.at[0, at, source], core_sem.at[1, at, source], sibling)

    def settle(slot, at):
        for source in range(nq):
            here = slot(1 - c, source)
            remote(here, here, core_sem.at[0, at, 0], core_sem.at[1, at, source], sibling).wait_recv()

    def products(left, count, *tiles):
        rows = count * TILE

        def of_model(m):
            parts = [left[m, pl.ds(tile, count)].reshape(rows, width) for tile in tiles]
            return jnp.dot(jnp.concatenate(parts, axis=0), w_ref[m], preferred_element_type=F32)

        total = of_model(0) + of_model(1)
        for number, tile in enumerate(tiles):
            prod[pl.ds(tile, count)] = total[number * rows : (number + 1) * rows].reshape(count, TILE, nlat)

    def turned(left, right):
        for m in range(2):
            right[m] = left[m].reshape(nt * TILE, width).T

    piece = nlat // 2
    pieces = 2 * nt

    def half_of(k):
        return pl.ds(pl.multiple_of(lax.rem(k, 2) * piece, piece), piece)

    def chain(bufs, sems, order, on_total):
        right_in, right_out, left_in, left_out = bufs

        def to_right(k):
            return remote(right_out.at[k], right_in.at[k], sems.at[0, k], sems.at[1, k], after)

        def to_left(k):
            return remote(left_out.at[k], left_in.at[k], sems.at[2, k], sems.at[3, k], before)

        def steps(low, high, on_step=None):
            @pl.loop(low, high)
            def _(step):
                right, left, done = step - SKEW * f, step - SKEW * (last - f), step - lag

                @pl.when((right >= 0) & (right < pieces))
                def _():
                    tile, k, cols = order(right)

                    @pl.when(f > 0)
                    def _():
                        to_right(k).wait_recv()

                    @pl.when(f < last)
                    def _():
                        right_out[k] = (prod[tile, :, cols] + right_in[k].astype(F32)).astype(BF16)
                        to_right(k).start()

                @pl.when((left >= 0) & (left < pieces))
                def _():
                    tile, k, cols = order(left)

                    @pl.when(f < last)
                    def _():
                        to_left(k).wait_recv()

                    @pl.when(f > 0)
                    def _():
                        left_out[k] = (prod[tile, :, cols] + left_in[k].astype(F32)).astype(BF16)
                        to_left(k).start()

                @pl.when((done >= 0) & (done < pieces))
                def _():
                    tile, k, cols = order(done)
                    on_total(tile, cols, prod[tile, :, cols] + right_in[k].astype(F32) + left_in[k].astype(F32))

                if on_step is not None:
                    on_step(step)

        def drain():
            @pl.loop(0, pieces)
            def _(k):
                @pl.when(f < last)
                def _():
                    to_right(k).wait_send()

                @pl.when(f > 0)
                def _():
                    to_left(k).wait_send()

        return steps, drain

    far = 1 - h

    def raw_slot(side):
        return lambda core, source: raw.at[side, core, source]

    def unpack(side):
        rows = TILE // 2

        @pl.loop(0, nq)
        def _(source):
            first, second = raw[side, 0, source].astype(F32), raw[side, 1, source].astype(F32)
            tile = (source // per) * 2 * per + side * per + lax.rem(source, per)
            for m in range(2):
                part = slice(m * rows, (m + 1) * rows)
                xs[m, tile] = jnp.concatenate([first[part], second[part]], axis=0).astype(BF16)

    start(a_ref, raw.at[h, c, q], h_sem.at[0, 0], h_sem.at[1, 0], partner)
    spread(a_ref, raw_slot(h), 0)
    w_copy.wait()
    for m in range(2):
        wt[m] = w_ref[m].T
    collect(raw_slot(h), 0)
    far_here = raw.at[far, c, q]
    remote(far_here, far_here, h_sem.at[0, 0], h_sem.at[1, 0], partner).wait_recv()
    spread(far_here, raw_slot(far), 1)
    settle(raw_slot(h), 0)
    unpack(h)
    products(xs, per, h * per, (2 + h) * per)

    def activate(k, cols, total):
        pre = total + eb_ref[:, cols]
        fall = jnp.exp(-jnp.abs(pre))
        lats[k, :, cols] = (jnp.maximum(pre, 0.0) + jnp.log1p(fall)).astype(BF16)
        sig[k, :, cols] = jnp.where(pre >= 0, 1.0, fall) / (1.0 + fall)

    def own_first(number):
        k = number // 2
        late, turn = k // (4 * per), lax.rem(k // per, 4)
        side = jnp.where(late == 0, turn // 2, lax.rem(turn, 2))
        group = jnp.where(late == 0, lax.rem(turn, 2), turn // 2 + 2 * late)
        tile = group * 2 * per + lax.rem(side + h, 2) * per + lax.rem(k, per)
        return tile, 2 * tile + lax.rem(number, 2), half_of(number)

    steps, drain = chain((sr, ss, tl, ts), line_sem, own_first, activate)
    steps(0, nq - 2)
    collect(raw_slot(far), 1)
    steps(nq - 2, nq)
    settle(raw_slot(far), 1)
    unpack(far)
    products(xs, per, far * per, (2 + far) * per)
    steps(nq, nq + nq // 4)
    products(xs, nq, nq)

    def terms(tile, m):
        return lax.dot_general(
            lats[pl.ds(tile, per)].reshape(per * TILE, nlat), wt[m],
            (((1,), (0,)), ((), ())), preferred_element_type=F32,
        ).reshape(per, TILE, width)

    def recon(g):
        for m in range(2):
            half_out[g, m] = terms((2 * g + 1 - c) * per, m).astype(BF16)
        start(half_out.at[g], half_in.at[g], half_sem.at[0, g], half_sem.at[1, g], sibling)
        for m in range(2):
            half_own[g, m] = terms((2 * g + c) * per, m)

    part_width = width // split

    def block_of(owner):
        first = pl.multiple_of(lax.rem(owner, split) * part_width, part_width)
        return lax.rem(owner // split, 2), owner // (2 * split), pl.ds(first, part_width)

    def own_part(g, owner):
        m, tile, chan = block_of(owner)
        return half_own[g, m, tile, :, chan] + half_in[g, m, tile, :, chan].astype(F32)

    def scatter(g):
        remote(
            half_out.at[g], half_in.at[g], half_sem.at[0, g], half_sem.at[1, g], sibling
        ).wait_recv()
        for number, (dy, dx) in enumerate(offsets):
            py, px = at_offset(dy, dx)
            part_out[g, number] = own_part(g, py * nx + px).astype(BF16)
            start(
                part_out.at[g, number], part_in.at[g, number],
                xy_sem.at[0, 2 + GROUPS + g, number], xy_sem.at[1, 2 + GROUPS + g, number], (f, py, h, px, c),
            )

    def pair_up(g):
        total = own_part(g, q)
        for number in range(len(offsets)):
            here = part_in.at[g, number]
            remote(here, here, xy_sem.at[0, 2 + GROUPS + g, number], xy_sem.at[1, 2 + GROUPS + g, number], sibling).wait_recv()
            total = total + part_in[g, number].astype(F32)
        pair_out[g] = total.astype(BF16)
        start(pair_out.at[g], pair_in.at[g], h_sem.at[0, 1 + g], h_sem.at[1, 1 + g], partner)

    def res_slot(g):
        def slot(core, source):
            m, tile, chan = block_of(source)
            return res.at[m, (2 * g + core) * per + tile, :, chan]

        return slot

    def residual(g):
        here = pair_in.at[g]
        remote(here, here, h_sem.at[0, 1 + g], h_sem.at[1, 1 + g], partner).wait_recv()
        m, tile, chan = block_of(q)
        tile = (2 * g + c) * per + tile
        bias = jnp.where(m == 0, db_ref[0:1, chan], db_ref[1:2, chan])
        summed = pair_out[g].astype(F32) + pair_in[g].astype(F32)
        res[m, tile, :, chan] = (scale * summed + bias - xs[m, tile, :, chan].astype(F32)).astype(BF16)
        spread(res_slot(g)(c, q), res_slot(g), 2 + g)

    def gather(g):
        collect(res_slot(g), 2 + g)

    def arrived(g):
        settle(res_slot(g), 2 + g)
        products(res, 2 * per, 2 * g * per)

    def run(low, base, plan, high):
        for at, stage, g in plan:
            steps(low, base + at)
            stage(g)
            low = base + at
        steps(low, high)

    ready = nt + lag
    first = 6 * per
    run(nq + nq // 4, lag, [
        (first, recon, 0), (first + nq // 4, scatter, 0), (8 * per, recon, 1), (8 * per + nq // 4, scatter, 1),
        (10 * per + nq // 8, pair_up, 0), (12 * per, recon, 2), (12 * per + nq // 8, pair_up, 1),
        (13 * per, scatter, 2), (15 * per + nq // 8, residual, 0),
    ], pieces + lag)
    recon(3)
    pair_up(2)
    scatter(3)
    residual(1)
    turned(xs, xt)
    gather(0)
    arrived(0)

    below = nq * TILE

    def dec_block(number):
        m, cols = number // 2, half_of(number)
        acc[m, :, cols] = scale * jnp.dot(
            rt[m], lats[:, :, cols].reshape(nt * TILE, piece), preferred_element_type=F32
        )

    def enc_block(number):
        m, cols = number // 2, half_of(number)
        acc[m, :, cols] += jnp.dot(
            xt[m, :, :below], grads[:nq, :, cols].reshape(below, piece), preferred_element_type=F32
        )

    def blocks_from(low, block):
        def on_step(step):
            @pl.when(step - low < 4)
            def _():
                block(step - low)

        return on_step

    def finish(k, cols, total):
        grad = scale * total * sig[k, :, cols]
        grads[k, :, cols] = grad.astype(BF16)
        gacc[:, cols] += grad

    steps, drain2 = chain(
        (sr2, ss2, tl2, ts2), line2_sem, lambda number: (number // 2, number, half_of(number)), finish
    )
    run(0, 0, [
        (nq // 8, pair_up, 3), (nq // 4 + nq // 8, gather, 1), (nq // 4 + nq // 8, residual, 2), (2 * per, arrived, 1),
        (5 * per + nq // 8, gather, 2), (5 * per + nq // 8, residual, 3), (6 * per, arrived, 2),
        (9 * per + nq // 8, gather, 3), (10 * per, arrived, 3),
    ], 10 * per)
    turned(res, rt)
    for m in range(2):
        gdb_ref[m : m + 1] = jnp.sum(jnp.sum(res[m].astype(F32), axis=0), axis=0, keepdims=True)
    steps(10 * per, ready, blocks_from(10 * per, dec_block))
    steps(ready, ready + 4, blocks_from(ready, enc_block))
    outs = [
        pltpu.make_async_copy(acc, acc_out, out_sem.at[0]),
        pltpu.make_async_copy(xt.at[:, :, pl.ds(below, below)], xt_out, out_sem.at[1]),
        pltpu.make_async_copy(grads.at[pl.ds(nq, nq)], grads_out, out_sem.at[2]),
    ]
    outs[0].start()
    outs[1].start()
    steps(ready + 4, pieces + lag)
    outs[2].start()

    def to_chip(ahead):
        return remote(
            gebuf, gebuf, geb_send.at[ahead], geb_recv.at[0], (lax.rem(mid + ahead, nf), y, h, x, c)
        )

    @pl.when(f == mid)
    def _():
        gebuf[...] = jnp.broadcast_to(jnp.sum(gacc[...], axis=0, keepdims=True), gebuf.shape)
        for ahead in range(1, nf):
            to_chip(ahead).start()

    drain()
    drain2()
    for copy in sent:
        copy.wait_send()

    @pl.when(f == mid)
    def _():
        for ahead in range(1, nf):
            to_chip(ahead).wait_send()

    @pl.when(f != mid)
    def _():
        to_chip(1).wait_recv()

    geb_ref[...] = gebuf[0:1]
    for copy in outs:
        copy.wait()


def last_product(acc_ref, xt_ref, grads_ref, geb_in, gdb_in, gw_ref, geb_ref, gdb_ref):
    rest = jnp.dot(xt_ref[0], grads_ref[...], preferred_element_type=F32)
    gw_ref[0] = (acc_ref[0] + rest).astype(BF16)
    geb_ref[...] = geb_in[...]
    gdb_ref[...] = gdb_in[...]


def on_device(sizes, acts, weight, enc_bias, dec_bias):
    nf, ny, nh, nx, nc = sizes
    lat_count = ny * nh * nx * nc
    _, width, nlat = weight.shape
    scale = math.sqrt(2.0 * (width * nf) / (nlat * lat_count))
    nq = ny * nx
    nt, per = 2 * nq, nq // GROUPS
    vmem = pltpu.VMEM
    tiles = vmem((2, nt, TILE, width), BF16)
    chunk = vmem((nt, TILE, nlat), BF16)
    wide = vmem((nt, TILE, nlat), F32)
    flow = vmem((2 * nt, TILE, nlat // 2), BF16)
    turned = vmem((2, width, nt * TILE), BF16)
    half = vmem((GROUPS, 2, per, TILE, width), BF16)
    pair = vmem((GROUPS, TILE, 2 * width // GROUPS), BF16)
    parts = vmem((GROUPS, nq - 1, TILE, 2 * width // GROUPS), BF16)
    dma = pltpu.SemaphoreType.DMA
    whole = pl.BlockSpec(memory_space=pltpu.VMEM)
    anywhere = pl.BlockSpec(memory_space=pl.ANY)
    below = nq * TILE
    acc, xt, grads, geb, gdb = pl.pallas_call(
        functools.partial(chain_kernel, sizes, scale),
        out_shape=(
            jax.ShapeDtypeStruct((2, width, nlat), F32),
            jax.ShapeDtypeStruct((2, width, below), BF16),
            jax.ShapeDtypeStruct((nq, TILE, nlat), BF16),
            jax.ShapeDtypeStruct((1, nlat), F32),
            jax.ShapeDtypeStruct((2, width), F32),
        ),
        in_specs=[whole, pl.BlockSpec(memory_space=pl.ANY), whole, whole],
        out_specs=(anywhere, anywhere, anywhere, whole, whole),
        scratch_shapes=[
            vmem((2, width, nlat), BF16), vmem((2, nlat, width), BF16), vmem((2, 2, nq, TILE, width), BF16),
            tiles, turned, turned, wide, wide, chunk, chunk, tiles,
            *([flow] * 8),
            half, half, vmem((GROUPS, 2, per, TILE, width), F32), parts, parts, pair, pair,
            vmem((2, width, nlat), F32), vmem((TILE, nlat), F32), vmem((8, nlat), F32),
            dma, dma((2, 1 + GROUPS)), dma((2, GROUPS)), dma((2, 2 + 2 * GROUPS, nq)), dma((2, 2 + GROUPS, nq)), dma((4, 2 * nt)), dma((4, 2 * nt)),
            dma((nf,)), dma((1,)), dma((3,)),
        ],
        compiler_params=pltpu.CompilerParams(
            collective_id=0, has_side_effects=True, vmem_limit_bytes=60 * 1024 * 1024
        ),
        name="crosscoder_step",
    )(acts.reshape(TILE, width), weight, enc_bias.reshape(1, nlat), dec_bias)
    cols = nlat // 2
    grad_weight, grad_enc, grad_dec = pl.pallas_call(
        last_product,
        out_shape=(
            jax.ShapeDtypeStruct((2, width, nlat), BF16),
            jax.ShapeDtypeStruct((1, nlat), F32),
            jax.ShapeDtypeStruct((2, width), F32),
        ),
        grid=(2, 2),
        in_specs=[
            pl.BlockSpec((1, width, cols), lambda m, n: (m, 0, n)),
            pl.BlockSpec((1, width, below), lambda m, n: (m, 0, 0)),
            pl.BlockSpec((below, cols), lambda m, n: (0, n)),
            pl.BlockSpec((1, nlat), lambda m, n: (0, 0)),
            pl.BlockSpec((2, width), lambda m, n: (0, 0)),
        ],
        out_specs=(
            pl.BlockSpec((1, width, cols), lambda m, n: (m, 0, n)),
            pl.BlockSpec((1, nlat), lambda m, n: (0, 0)),
            pl.BlockSpec((2, width), lambda m, n: (0, 0)),
        ),
        name="last_product",
    )(acc, xt, grads.reshape(below, nlat), geb, gdb)
    return grad_weight, grad_enc.reshape(nlat), grad_dec


def solution(mesh):
    shape = dict(mesh.shape)
    if shape["lat"] == 64:
        sizes = (shape["feat"], 4, 2, 4, 2)
    else:
        sizes = (shape["feat"], 1, 2, shape["lat"] // 4, 2)
    torus = Mesh(mesh.devices.reshape(sizes), AXES)
    in_specs = (P(None, LAT, "feat"), P(None, "feat", LAT), P(LAT), P(None, "feat"))
    out_specs = (P(None, "feat", LAT), P(LAT), P(None, "feat"))
    return jax.shard_map(
        functools.partial(on_device, sizes),
        mesh=torus, in_specs=in_specs, out_specs=out_specs, check_vma=False,
    )
```
